512 devices in a mesh: tm: 32 (over x, y), user: 16 (over z, core).
Axes of the slice: x: 4, y: 8, z: 8, core: 2. Of those that a mesh axis runs over, the one named last changes fastest.
Arguments:
- events: bfloat16 [16, 32768, 512], P('user', 'tm'), may hold values from -6 to 6
- w_first: bfloat16 [512, 1024], replicated, may hold values from -0.25 to 0.25
- b_first: float32 [1024], replicated, may hold values from -3 to 3
- w_second: bfloat16 [1024, 512], replicated, may hold values from -0.1875 to 0.1875
- count_embed: float32 [512], replicated, may hold values from -0.3 to 0.3
- norm_gain: float32 [512], replicated, may hold values from 0.5 to 1.5
- event_session: int32 [16, 32768], P('user', 'tm'), may hold values from 0 to 2047, as said below
- event_count: int32 [16, 32], P('user', 'tm'), may hold values from 256 to 1024, as said below
- session_user: int32 [16, 2048], P('user', 'tm'), may hold values from 0 to 65535, as said below
Outputs:
- section_rows: bfloat16 [32, 16, 128, 512], P('tm', 'user')
- section_users: int32 [32, 16, 128], P('tm', 'user')
The draws below stay inside these ranges and needn't reach their ends.
Inputs may be any that keep to these rules, and one draw needn't show every extreme that they name: `event_session`: the events of time slice t (slots t * 1024 to (t + 1) * 1024 - 1 of a shard) name sessions of slices max(0, t - 16) to t only; some sessions have no valid event. `event_count`: some time slice of some shard has all 1024 events valid. `session_user`: among the 64 sessions of one shard and time slice, at most 8 have users of the same section (user mod 16); in every time slice some section gets exactly 8 from every shard.
All inputs are finite; a program needn't handle non-finite values.
Results may differ from the reference program's by a relative error of at most 0.0042.
Values may be sent and summed in bfloat16 or wider, within the bound.
No kernel may reach another device: no remote copies, remote signals or barrier semaphores. Data moves between devices by JAX's collectives and lax.ppermute only.
A program may use at most 64 MiB of HBM per device.

```python
import jax
import jax.numpy as jnp
from jax import lax

D = 512
FF = 1024
EV_DEV = 1024
SESS_DEV = 64
USERS = 65536
SECTIONS = 16
SESS_G = 2048
EVENTS_G = 32768
CAP = 8
N_TM = 32
N_USER = 16


def draw_event_count(key, part):
    slices = SESS_G // SESS_DEV
    key_count, key_fullest = jax.random.split(jax.random.fold_in(key, 11))
    counts = jax.random.randint(key_count, (SECTIONS * slices,), EV_DEV // 4, EV_DEV + 1)
    fullest = jax.random.randint(key_fullest, (), 0, SECTIONS * slices)
    flattened = jnp.where(jnp.arange(SECTIONS * slices) == fullest, EV_DEV, counts)
    return flattened.reshape(SECTIONS, slices).astype(jnp.int32)


def draw_event_session(key, part):
    slices = SESS_G // SESS_DEV
    half_reach = slices // 2
    key_dead, key_offset = jax.random.split(jax.random.fold_in(key, 23))
    alive_table = jax.random.randint(key_dead, (SECTIONS, SESS_G), 0, 6) != 0
    slice_of = jnp.arange(slices * EV_DEV, dtype=jnp.int32) // EV_DEV
    first_slice = jnp.maximum(slice_of - half_reach, 0)
    span = (slice_of - first_slice + 1) * SESS_DEV
    offsets = jax.random.randint(key_offset, (4, SECTIONS, slices * EV_DEV), 0, 2 ** 30) % span
    candidate = first_slice * SESS_DEV + offsets
    chosen = candidate[3]
    for attempt in (2, 1, 0):
        living = jnp.take_along_axis(alive_table, candidate[attempt], axis=1)
        chosen = jnp.where(living, candidate[attempt], chosen)
    return chosen.astype(jnp.int32)


def draw_session_user(key, part):
    slices = SESS_G // SESS_DEV
    width = SECTIONS * CAP
    slots = jnp.arange(width)
    block_keys = jax.random.split(jax.random.fold_in(key, 41), SECTIONS * slices)
    first_slice = jax.random.randint(jax.random.fold_in(key, 43), (slices,), 0, SECTIONS)
    first_column = jnp.tile(first_slice, SECTIONS)

    def arrange(block_key, column_full):
        key_slot, key_place, key_member = jax.random.split(block_key, 3)
        scores = jax.random.randint(key_slot, (width,), 0, 2 ** 20) * width + slots
        scores = jnp.where(slots // CAP == column_full, slots - width, scores)
        order = jnp.argsort(scores)
        columns = order[:SESS_DEV] // CAP
        placing = jax.random.randint(key_place, (SESS_DEV,), 0, 2 ** 20) * SESS_DEV + jnp.arange(SESS_DEV)
        columns = columns[jnp.argsort(placing)]
        member = jax.random.randint(key_member, (SESS_DEV,), 0, USERS // SECTIONS)
        return columns + SECTIONS * member
    result = jax.vmap(arrange)(block_keys, first_column)
    return result.reshape(SECTIONS, slices * SESS_DEV).astype(jnp.int32)


def steps_of(stream_key, extent, cuts, least, high):
    loudness = 1.0
    for position, blocks in cuts:
        draws = jax.random.uniform(jax.random.fold_in(jax.random.fold_in(stream_key, 6), position), (blocks,), jnp.float32, least / len(cuts), high / len(cuts))
        loudness = loudness * jnp.repeat(jnp.exp(draws), extent[position] // blocks).reshape((-1,) + (1,) * (len(extent) - 1 - position))
    return loudness


def gaussian(stream_key, shape, spread, reach, pieces=(), held_as=jnp.bfloat16):
    entries = spread * jax.random.normal(stream_key, shape, jnp.float32)
    if pieces:
        entries = entries * steps_of(stream_key, shape, pieces, -0.22, 0.18)
    return jnp.clip(entries, -reach, reach).astype(held_as)


def setup_inputs(seed: int = 0) -> dict:
    splits = jax.random.split(jax.random.key(seed), 10)
    return {
        "events": gaussian(splits[0], (N_USER, EVENTS_G, D), 1.0, 6.0, ((0, 16), (1, 32))),
        "w_first": gaussian(splits[1], (D, FF), D ** -0.5, 0.25),
        "b_first": gaussian(splits[2], (FF,), 0.5, 3.0, (), jnp.float32),
        "w_second": gaussian(splits[3], (FF, D), FF ** -0.5, 0.1875),
        "count_embed": gaussian(splits[4], (D,), 0.05, 0.3, (), jnp.float32),
        "norm_gain": jnp.clip(1.0 + 0.1 * jax.random.normal(splits[5], (D,), jnp.float32), 0.5, 1.5),
        "event_session": draw_event_session(jax.random.fold_in(splits[9], 71), 0),
        "event_count": draw_event_count(jax.random.fold_in(splits[9], 71), 0),
        "session_user": draw_session_user(jax.random.fold_in(splits[9], 71), 0),
    }


def embed(event_rows, w_first, b_first, w_second):
    hidden = jax.nn.gelu(jnp.dot(event_rows, w_first, preferred_element_type=jnp.float32) + b_first).astype(jnp.bfloat16)
    return jnp.dot(hidden, w_second, preferred_element_type=jnp.float32).astype(jnp.bfloat16)

def reference(events, w_first, b_first, w_second, count_embed, norm_gain, event_session, event_count, session_user):

    def shard_sums(packed):
        event_rows, session_ids, slice_counts = packed
        vectors = embed(event_rows, w_first, b_first, w_second).astype(jnp.float32)
        within = jnp.arange(N_TM * EV_DEV) % EV_DEV
        valid = within < jnp.repeat(slice_counts, EV_DEV)
        target = jnp.where(valid, session_ids, SESS_G)
        sums = jax.ops.segment_sum(vectors, target, SESS_G + 1)[:SESS_G]
        totals = jax.ops.segment_sum(valid.astype(jnp.float32), target, SESS_G + 1)[:SESS_G]
        return (sums, totals)
    sums, totals = lax.map(shard_sums, (events, event_session, event_count))
    averaged = sums / jnp.maximum(totals, 1.0)[..., None]
    mixed = averaged + jnp.log1p(totals)[..., None] * count_embed
    scaled = mixed * lax.rsqrt(lax.optimization_barrier(jnp.mean(mixed * mixed, axis=-1, keepdims=True)) + 1e-06) * norm_gain
    session_rows = scaled.astype(jnp.bfloat16).reshape(N_USER, N_TM, SESS_DEV, D)
    users = session_user.reshape(N_USER, N_TM, SESS_DEV)
    section = users % N_USER
    same = section[..., :, None] == section[..., None, :]
    before = jnp.arange(SESS_DEV)[:, None] > jnp.arange(SESS_DEV)[None, :]
    rank = lax.optimization_barrier(jnp.sum((same & before).astype(jnp.int32), axis=-1))
    slot = section * CAP + rank
    assign = slot[..., None, :] == jnp.arange(N_USER * CAP)[:, None]
    placed = jnp.einsum('utcs,utsd->tucd', assign.astype(jnp.float32), session_rows.astype(jnp.float32))
    placed = placed.reshape(N_TM, N_USER, N_USER, CAP, D).transpose(0, 2, 1, 3, 4)
    section_rows = placed.reshape(N_TM, N_USER, N_USER * CAP, D).astype(jnp.bfloat16)
    slot_users = lax.optimization_barrier(jnp.sum(jnp.where(assign, users[..., None, :] + 1, 0), axis=-1)) - 1
    slot_users = slot_users.reshape(N_USER, N_TM, N_USER, CAP).transpose(1, 2, 0, 3)
    section_users = slot_users.reshape(N_TM, N_USER, N_USER * CAP).astype(jnp.int32)
    return (section_rows, section_users)
```

```python
import functools

import jax
import jax.numpy as jnp
from jax import lax
from jax.experimental import pallas as pl
from jax.experimental.pallas import tpu as pltpu
from jax.sharding import PartitionSpec as P

LANES = 128
DIGIT = 256.0


def count_tile(row):
    high = jnp.floor(row * (1.0 / DIGIT))
    low = row - high * DIGIT
    at = lax.broadcasted_iota(jnp.int32, (8, LANES), 0)
    return jnp.where(at == 0, high, jnp.where(at == 1, low, 0.0))


def embed_kernel(window, sess, count_ref, ev_ref, w1_ref, b1_ref, w2_ref, ids_ref, out_ref, far_ref, vec, acc):
    rows, width = ev_ref.shape
    groups = width // LANES
    pick = window * sess
    t = lax.axis_index("tm")
    step = 256
    for c in range(rows // step):
        at = pl.ds(c * step, step)
        h = jnp.dot(ev_ref[at, :], w1_ref[...], preferred_element_type=jnp.float32)
        h = jax.nn.gelu(h + b1_ref[...]).astype(jnp.bfloat16)
        vec[at, :width] = jnp.dot(h, w2_ref[...], preferred_element_type=jnp.float32).astype(jnp.bfloat16)
        vec[at, width:] = jnp.ones((step, LANES), jnp.bfloat16)
    ids = ids_ref[...]
    far = (ids // sess) == t - window
    target = jnp.where(far, pick + ids % LANES, ids % pick)
    valid = lax.broadcasted_iota(jnp.int32, ids.shape, 1) < count_ref[0, 0]
    target = jnp.where(valid, target, -1)
    total = pick + LANES
    onehot = lax.broadcasted_iota(jnp.int32, (total, rows), 0) == target
    acc[...] = jnp.dot(
        jnp.where(onehot, 1.0, 0.0).astype(jnp.bfloat16), vec[...], preferred_element_type=jnp.float32
    )
    eye = lax.broadcasted_iota(jnp.int32, (LANES, LANES), 0) == lax.broadcasted_iota(
        jnp.int32, (LANES, LANES), 1
    )
    per = LANES // sess
    for c in range(total // LANES):
        counted = acc[c * LANES : (c + 1) * LANES, width:]
        tile = count_tile(jnp.sum(jnp.where(eye, counted, 0.0), axis=0, keepdims=True)).astype(jnp.bfloat16)
        if c < pick // LANES:
            for b in range(per):
                r = c * per + b
                for g in range(groups):
                    out_ref[r, g * sess : (g + 1) * sess, :] = acc[
                        r * sess : (r + 1) * sess, g * LANES : (g + 1) * LANES
                    ].astype(jnp.bfloat16)
                out_ref[r, groups * sess :, :] = tile
        else:
            start = pl.multiple_of(pick + sess * lax.rem(t, per), sess)
            for g in range(groups):
                far_ref[g * sess : (g + 1) * sess, :] = acc[
                    pl.ds(start, sess), g * LANES : (g + 1) * LANES
                ].astype(jnp.bfloat16)
            far_ref[groups * sess :, :] = tile


def far_kernel(window, recv_ref, far_ref, out_ref):
    me = lax.rem(lax.axis_index("tm"), window)
    total = far_ref[...].astype(jnp.float32)
    for j in range(window - 1):
        total += jnp.where(j < me, recv_ref[j].astype(jnp.float32), 0.0)
    data = total.shape[0] - 8
    out_ref[:data, :] = total[:data].astype(jnp.bfloat16)
    out_ref[data:, :] = count_tile(DIGIT * total[data : data + 1] + total[data + 1 : data + 2]).astype(jnp.bfloat16)


def near_kernel(window, recv_ref, out_ref):
    me = lax.rem(lax.axis_index("tm"), window)
    total = recv_ref[window - 1].astype(jnp.float32)
    for j in range(window - 1):
        total += jnp.where(j >= me, recv_ref[j].astype(jnp.float32), 0.0)
    out_ref[...] = total


def pack_kernel(n_sec, near_ref, got_ref, embed_ref, gain_ref, users_ref, out_ref):
    sess = users_ref.shape[1]
    width = embed_ref.shape[1]
    groups = width // LANES
    slots = out_ref.shape[0]
    capacity = slots // n_sec
    t = lax.axis_index("tm")
    total = near_ref[...] + got_ref[...].astype(jnp.float32)
    data = groups * sess
    counts = DIGIT * total[data : data + 1] + total[data + 1 : data + 2]
    spot = lax.broadcasted_iota(jnp.int32, (sess, LANES), 0) + sess * lax.rem(t, LANES // sess)
    mine = spot == lax.broadcasted_iota(jnp.int32, (sess, LANES), 1)
    counts = jnp.sum(jnp.where(mine, counts, 0.0), axis=1, keepdims=True)
    least = jnp.maximum(counts, 1.0)
    weight = jnp.log1p(counts)
    mixed = [
        total[g * sess : (g + 1) * sess] / least + weight * embed_ref[:, g * LANES : (g + 1) * LANES]
        for g in range(groups)
    ]
    square = sum(m * m for m in mixed)
    scale = lax.rsqrt(jnp.sum(square, axis=1, keepdims=True) / width + 1e-06)
    session_rows = jnp.concatenate(
        [(m * scale * gain_ref[:, g * LANES : (g + 1) * LANES]).astype(jnp.bfloat16) for g, m in enumerate(mixed)],
        axis=1,
    )
    users = users_ref[...]
    section = lax.rem(users, n_sec)
    i0 = lax.broadcasted_iota(jnp.int32, (sess, sess), 0)
    i1 = lax.broadcasted_iota(jnp.int32, (sess, sess), 1)
    section_column = jnp.sum(jnp.where(i0 == i1, section, 0), axis=1, keepdims=True)
    rank = jnp.sum(jnp.where((section_column == section) & (i0 < i1), 1, 0), axis=0, keepdims=True)
    slot = section * capacity + rank
    assign = lax.broadcasted_iota(jnp.int32, (slots, sess), 0) == slot
    placed = jnp.dot(
        jnp.where(assign, 1.0, 0.0).astype(jnp.bfloat16), session_rows, preferred_element_type=jnp.float32
    )
    out_ref[:, :width] = placed.astype(jnp.bfloat16)
    named = jnp.sum(jnp.where(assign, (users + 1).astype(jnp.float32), 0.0), axis=1, keepdims=True)
    high = jnp.floor(named * (1.0 / DIGIT))
    low = named - high * DIGIT
    lane = lax.broadcasted_iota(jnp.int32, (slots, LANES), 1)
    out_ref[:, width:] = jnp.where(lane == 0, high, jnp.where(lane == 1, low, 0.0)).astype(jnp.bfloat16)


def unpack_kernel(got_ref, rows_ref, users_ref):
    slots = got_ref.shape[0]
    width = rows_ref.shape[1]
    rows_ref[...] = got_ref[:, :width]
    digits = got_ref[:, width:].astype(jnp.float32)
    lane = lax.broadcasted_iota(jnp.int32, digits.shape, 1)
    column = jnp.sum(jnp.where(lane == 0, DIGIT * digits, jnp.where(lane == 1, digits, 0.0)), axis=1, keepdims=True)
    eye = lax.broadcasted_iota(jnp.int32, (slots, slots), 0) == lax.broadcasted_iota(jnp.int32, (slots, slots), 1)
    users_ref[...] = jnp.sum(jnp.where(eye, column, 0.0), axis=0, keepdims=True).astype(jnp.int32) - 1


def on_device(
    events,
    w_first,
    b_first,
    w_second,
    count_embed,
    norm_gain,
    event_session,
    event_count,
    session_user,
):
    rows, width = events.shape[1:]
    sess = session_user.shape[1]
    n_tm = lax.axis_size("tm")
    n_sec = lax.axis_size("user")
    capacity = max(2, 2 * sess // n_sec)
    window = n_tm // 2
    block = width // LANES * sess + 8
    bf16, f32 = jnp.bfloat16, jnp.float32
    vmem = pl.BlockSpec(memory_space=pltpu.VMEM)
    smem = pl.BlockSpec(memory_space=pltpu.SMEM)
    shape = jax.ShapeDtypeStruct
    blocks, far = pl.pallas_call(
        functools.partial(embed_kernel, window, sess),
        out_shape=(shape((window, block, LANES), bf16), shape((block, LANES), bf16)),
        in_specs=[smem] + [vmem] * 5,
        out_specs=(vmem, vmem),
        scratch_shapes=[
            pltpu.VMEM((rows, width + LANES), bf16),
            pltpu.VMEM((window * sess + LANES, width + LANES), f32),
        ],
        name="embed",
    )(event_count, events[0], w_first, b_first[None], w_second, event_session)
    groups = [[first + j for j in range(window)] for first in range(0, n_tm, window)]
    arrived = lax.all_to_all(blocks, "tm", 0, 0, tiled=True, axis_index_groups=groups)
    far = pl.pallas_call(
        functools.partial(far_kernel, window),
        out_shape=shape((block, LANES), bf16),
        in_specs=[vmem, vmem],
        out_specs=vmem,
        name="far",
    )(arrived, far)
    got = lax.ppermute(far, "tm", [(t, t - window) for t in range(window, n_tm)])
    near = pl.pallas_call(
        functools.partial(near_kernel, window),
        out_shape=shape((block, LANES), f32),
        in_specs=[vmem],
        out_specs=vmem,
        name="near",
    )(arrived)
    outgoing = pl.pallas_call(
        functools.partial(pack_kernel, n_sec),
        out_shape=shape((n_sec * capacity, width + LANES), bf16),
        in_specs=[vmem] * 5,
        out_specs=vmem,
        name="pack",
    )(near, got, count_embed[None], norm_gain[None], session_user)
    routed = lax.all_to_all(
        outgoing.reshape(n_sec, capacity, width + LANES), "user", 0, 0, tiled=True
    ).reshape(n_sec * capacity, width + LANES)
    section_rows, section_users = pl.pallas_call(
        unpack_kernel,
        out_shape=(shape((n_sec * capacity, width), bf16), shape((1, n_sec * capacity), jnp.int32)),
        in_specs=[vmem],
        out_specs=(vmem, vmem),
        name="unpack",
    )(routed)
    return (section_rows[None, None], section_users[None])


def solution(mesh):
    in_specs = (
        P("user", "tm", None),
        P(),
        P(),
        P(),
        P(),
        P(),
        P("user", "tm"),
        P("user", "tm"),
        P("user", "tm"),
    )
    out_specs = (P("tm", "user", None, None), P("tm", "user", None))
    return jax.shard_map(
        on_device, mesh=mesh, in_specs=in_specs, out_specs=out_specs, check_vma=False
    )
```

```python
import functools

import jax
import jax.numpy as jnp
from jax import lax
from jax.experimental import pallas as pl
from jax.experimental.pallas import tpu as pltpu
from jax.sharding import PartitionSpec as P

LANES = 128
DIGIT = 256.0


def count_tile(row):
    high = jnp.floor(row * (1.0 / DIGIT))
    low = row - high * DIGIT
    at = lax.broadcasted_iota(jnp.int32, (8, LANES), 0)
    return jnp.where(at == 0, high, jnp.where(at == 1, low, 0.0))


def embed_kernel(window, sess, count_ref, ev_ref, w1_ref, b1_ref, w2_ref, ids_ref, out_ref, far_ref, vec, acc):
    rows, width = ev_ref.shape
    groups = width // LANES
    pick = window * sess
    t = lax.axis_index("tm")
    step = 256
    for c in range(rows // step):
        at = pl.ds(c * step, step)
        h = jnp.dot(ev_ref[at, :], w1_ref[...], preferred_element_type=jnp.float32)
        h = jax.nn.gelu(h + b1_ref[...]).astype(jnp.bfloat16)
        vec[at, :width] = jnp.dot(h, w2_ref[...], preferred_element_type=jnp.float32).astype(jnp.bfloat16)
        vec[at, width:] = jnp.ones((step, LANES), jnp.bfloat16)
    ids = ids_ref[...]
    far = (ids // sess) == t - window
    target = jnp.where(far, pick + ids % LANES, ids % pick)
    valid = lax.broadcasted_iota(jnp.int32, ids.shape, 1) < count_ref[...]
    target = jnp.where(valid, target, -1)
    total = pick + LANES
    onehot = lax.broadcasted_iota(jnp.int32, (total, rows), 0) == target
    acc[...] = jnp.dot(
        jnp.where(onehot, 1.0, 0.0).astype(jnp.bfloat16), vec[...], preferred_element_type=jnp.float32
    )
    eye = lax.broadcasted_iota(jnp.int32, (LANES, LANES), 0) == lax.broadcasted_iota(
        jnp.int32, (LANES, LANES), 1
    )
    per = LANES // sess
    for c in range(total // LANES):
        counted = acc[c * LANES : (c + 1) * LANES, width:]
        tile = count_tile(jnp.sum(jnp.where(eye, counted, 0.0), axis=0, keepdims=True)).astype(jnp.bfloat16)
        if c < pick // LANES:
            for b in range(per):
                r = c * per + b
                for g in range(groups):
                    out_ref[r, g * sess : (g + 1) * sess, :] = acc[
                        r * sess : (r + 1) * sess, g * LANES : (g + 1) * LANES
                    ].astype(jnp.bfloat16)
                out_ref[r, groups * sess :, :] = tile
        else:
            start = pl.multiple_of(pick + sess * lax.rem(t, per), sess)
            for g in range(groups):
                far_ref[g * sess : (g + 1) * sess, :] = acc[
                    pl.ds(start, sess), g * LANES : (g + 1) * LANES
                ].astype(jnp.bfloat16)
            far_ref[groups * sess :, :] = tile


def far_kernel(window, recv_ref, far_ref, out_ref):
    me = lax.rem(lax.axis_index("tm"), window)
    total = far_ref[...].astype(jnp.float32)
    for j in range(window - 1):
        total += jnp.where(j < me, recv_ref[j].astype(jnp.float32), 0.0)
    data = total.shape[0] - 8
    out_ref[:data, :] = total[:data].astype(jnp.bfloat16)
    out_ref[data:, :] = count_tile(DIGIT * total[data : data + 1] + total[data + 1 : data + 2]).astype(jnp.bfloat16)


def near_kernel(window, recv_ref, out_ref):
    me = lax.rem(lax.axis_index("tm"), window)
    total = recv_ref[window - 1].astype(jnp.float32)
    for j in range(window - 1):
        total += jnp.where(j >= me, recv_ref[j].astype(jnp.float32), 0.0)
    out_ref[...] = total


def pack_kernel(n_sec, near_ref, got_ref, embed_ref, gain_ref, users_ref, out_ref):
    sess = users_ref.shape[1]
    width = embed_ref.shape[1]
    groups = width // LANES
    slots = out_ref.shape[0]
    capacity = slots // n_sec
    t = lax.axis_index("tm")
    total = near_ref[...] + got_ref[...].astype(jnp.float32)
    data = groups * sess
    counts = DIGIT * total[data : data + 1] + total[data + 1 : data + 2]
    spot = lax.broadcasted_iota(jnp.int32, (sess, LANES), 0) + sess * lax.rem(t, LANES // sess)
    mine = spot == lax.broadcasted_iota(jnp.int32, (sess, LANES), 1)
    counts = jnp.sum(jnp.where(mine, counts, 0.0), axis=1, keepdims=True)
    least = jnp.maximum(counts, 1.0)
    weight = jnp.log1p(counts)
    mixed = [
        total[g * sess : (g + 1) * sess] / least + weight * embed_ref[:, g * LANES : (g + 1) * LANES]
        for g in range(groups)
    ]
    square = sum(m * m for m in mixed)
    scale = lax.rsqrt(jnp.sum(square, axis=1, keepdims=True) / width + 1e-06)
    session_rows = jnp.concatenate(
        [(m * scale * gain_ref[:, g * LANES : (g + 1) * LANES]).astype(jnp.bfloat16) for g, m in enumerate(mixed)],
        axis=1,
    )
    users = users_ref[...]
    section = lax.rem(users, n_sec)
    i0 = lax.broadcasted_iota(jnp.int32, (sess, sess), 0)
    i1 = lax.broadcasted_iota(jnp.int32, (sess, sess), 1)
    section_column = jnp.sum(jnp.where(i0 == i1, section, 0), axis=1, keepdims=True)
    rank = jnp.sum(jnp.where((section_column == section) & (i0 < i1), 1, 0), axis=0, keepdims=True)
    slot = section * capacity + rank
    assign = lax.broadcasted_iota(jnp.int32, (slots, sess), 0) == slot
    placed = jnp.dot(
        jnp.where(assign, 1.0, 0.0).astype(jnp.bfloat16), session_rows, preferred_element_type=jnp.float32
    )
    out_ref[:, :width] = placed.astype(jnp.bfloat16)
    named = jnp.sum(jnp.where(assign, (users + 1).astype(jnp.float32), 0.0), axis=1, keepdims=True)
    high = jnp.floor(named * (1.0 / DIGIT))
    low = named - high * DIGIT
    lane = lax.broadcasted_iota(jnp.int32, (slots, LANES), 1)
    out_ref[:, width:] = jnp.where(lane == 0, high, jnp.where(lane == 1, low, 0.0)).astype(jnp.bfloat16)


def unpack_kernel(got_ref, rows_ref, users_ref):
    slots = got_ref.shape[0]
    width = rows_ref.shape[1]
    rows_ref[...] = got_ref[:, :width]
    digits = got_ref[:, width:].astype(jnp.float32)
    lane = lax.broadcasted_iota(jnp.int32, digits.shape, 1)
    column = jnp.sum(jnp.where(lane == 0, DIGIT * digits, jnp.where(lane == 1, digits, 0.0)), axis=1, keepdims=True)
    eye = lax.broadcasted_iota(jnp.int32, (slots, slots), 0) == lax.broadcasted_iota(jnp.int32, (slots, slots), 1)
    users_ref[...] = jnp.sum(jnp.where(eye, column, 0.0), axis=0, keepdims=True).astype(jnp.int32) - 1


def on_device(
    events,
    w_first,
    b_first,
    w_second,
    count_embed,
    norm_gain,
    event_session,
    event_count,
    session_user,
):
    rows, width = events.shape[1:]
    sess = session_user.shape[1]
    n_tm = lax.axis_size("tm")
    n_sec = lax.axis_size("user")
    capacity = max(2, 2 * sess // n_sec)
    window = n_tm // 2
    block = width // LANES * sess + 8
    bf16, f32 = jnp.bfloat16, jnp.float32
    vmem = pl.BlockSpec(memory_space=pltpu.VMEM)
    shape = jax.ShapeDtypeStruct
    kept = pltpu.VMEM
    pin = functools.partial(pltpu.with_memory_space_constraint, memory_space=pltpu.VMEM)
    blocks, far = pl.pallas_call(
        functools.partial(embed_kernel, window, sess),
        out_shape=(kept((window, block, LANES), bf16), kept((block, LANES), bf16)),
        in_specs=[vmem] * 6,
        out_specs=(vmem, vmem),
        scratch_shapes=[
            pltpu.VMEM((rows, width + LANES), bf16),
            pltpu.VMEM((window * sess + LANES, width + LANES), f32),
        ],
        name="embed",
    )(event_count, events[0], w_first, b_first[None], w_second, event_session)
    groups = [[first + j for j in range(window)] for first in range(0, n_tm, window)]
    arrived = lax.all_to_all(blocks, "tm", 0, 0, tiled=True, axis_index_groups=groups)
    far = pl.pallas_call(
        functools.partial(far_kernel, window),
        out_shape=kept((block, LANES), bf16),
        in_specs=[vmem, vmem],
        out_specs=vmem,
        name="far",
    )(pin(arrived), pin(far))
    got = lax.ppermute(far, "tm", [(t, t - window) for t in range(window, n_tm)])
    near = pl.pallas_call(
        functools.partial(near_kernel, window),
        out_shape=kept((block, LANES), f32),
        in_specs=[vmem],
        out_specs=vmem,
        name="near",
    )(pin(arrived))
    outgoing = pl.pallas_call(
        functools.partial(pack_kernel, n_sec),
        out_shape=kept((n_sec * capacity, width + LANES), bf16),
        in_specs=[vmem] * 5,
        out_specs=vmem,
        name="pack",
    )(pin(near), pin(got), count_embed[None], norm_gain[None], session_user)
    routed = lax.all_to_all(
        outgoing.reshape(n_sec, capacity, width + LANES), "user", 0, 0, tiled=True
    ).reshape(n_sec * capacity, width + LANES)
    section_rows, section_users = pl.pallas_call(
        unpack_kernel,
        out_shape=(shape((n_sec * capacity, width), bf16), shape((1, n_sec * capacity), jnp.int32)),
        in_specs=[vmem],
        out_specs=(vmem, vmem),
        name="unpack",
    )(pin(routed))
    return (section_rows[None, None], section_users[None])


def solution(mesh):
    in_specs = (
        P("user", "tm", None),
        P(),
        P(),
        P(),
        P(),
        P(),
        P("user", "tm"),
        P("user", "tm"),
        P("user", "tm"),
    )
    out_specs = (P("tm", "user", None, None), P("tm", "user", None))
    return jax.shard_map(
        on_device, mesh=mesh, in_specs=in_specs, out_specs=out_specs, check_vma=False
    )
```

```python
import functools

import jax
import jax.numpy as jnp
from jax import lax
from jax.experimental import pallas as pl
from jax.experimental.pallas import tpu as pltpu
from jax.sharding import PartitionSpec as P

LANES = 128
DIGIT = 256.0


def count_tile(row):
    high = jnp.floor(row * (1.0 / DIGIT))
    low = row - high * DIGIT
    at = lax.broadcasted_iota(jnp.int32, (8, LANES), 0)
    return jnp.where(at == 0, high, jnp.where(at == 1, low, 0.0))


def gelu(x):
    half = 0.5 * x
    inner = x * (0.7978845608028654 + 0.035677408136300125 * (x * x))
    return half + half * jnp.tanh(inner)


def embed_kernel(window, sess, step, count_ref, ev_ref, w1_ref, b1_ref, w2_ref, ids_ref, out_ref, far_ref, vec, acc, counted):
    rows, width = ev_ref.shape
    groups = width // LANES
    pick = window * sess
    t = lax.axis_index("tm")
    for c in range(rows // step):
        at = pl.ds(c * step, step)
        h = jnp.dot(ev_ref[at, :], w1_ref[...], preferred_element_type=jnp.float32)
        h = gelu(h + b1_ref[...]).astype(jnp.bfloat16)
        vec[at, :] = jnp.dot(h, w2_ref[...], preferred_element_type=jnp.float32).astype(jnp.bfloat16)
    ids = ids_ref[...]
    far = (ids // sess) == t - window
    target = jnp.where(far, pick + ids % sess, ids % pick)
    valid = lax.broadcasted_iota(jnp.int32, ids.shape, 1) < count_ref[0, 0]
    target = jnp.where(valid, target, -1)
    total = pick + sess
    onehot = jnp.where(lax.broadcasted_iota(jnp.int32, (total, rows), 0) == target, 1.0, 0.0)
    counted[...] = jnp.broadcast_to(jnp.sum(onehot, axis=1, keepdims=True), counted.shape)
    acc[...] = jnp.dot(onehot.astype(jnp.bfloat16), vec[...], preferred_element_type=jnp.float32)
    per = LANES // sess
    row = lax.broadcasted_iota(jnp.int32, (LANES, LANES), 0)
    lane = lax.broadcasted_iota(jnp.int32, (LANES, LANES), 1)
    for c in range(pick // LANES):
        found = jnp.where(row == lane, counted[c * LANES : (c + 1) * LANES, :], 0.0)
        tile = count_tile(jnp.sum(found, axis=0, keepdims=True)).astype(jnp.bfloat16)
        for r in range(c * per, (c + 1) * per):
            for g in range(groups):
                out_ref[r, g * sess : (g + 1) * sess, :] = acc[
                    r * sess : (r + 1) * sess, g * LANES : (g + 1) * LANES
                ].astype(jnp.bfloat16)
            out_ref[r, groups * sess :, :] = tile
    for g in range(groups):
        far_ref[g * sess : (g + 1) * sess, :] = acc[pick:, g * LANES : (g + 1) * LANES].astype(jnp.bfloat16)
    spot = row[:sess] + sess * lax.rem(t, per)
    found = jnp.where(spot == lane[:sess], counted[pick:, :], 0.0)
    far_ref[groups * sess :, :] = count_tile(jnp.sum(found, axis=0, keepdims=True)).astype(jnp.bfloat16)


def far_kernel(window, recv_ref, far_ref, out_ref):
    me = lax.rem(lax.axis_index("tm"), window)
    total = far_ref[...].astype(jnp.float32)
    for j in range(window - 1):
        total += jnp.where(j < me, recv_ref[j].astype(jnp.float32), 0.0)
    data = total.shape[0] - 8
    out_ref[:data, :] = total[:data].astype(jnp.bfloat16)
    out_ref[data:, :] = count_tile(DIGIT * total[data : data + 1] + total[data + 1 : data + 2]).astype(jnp.bfloat16)


def near_kernel(window, n_sec, recv_ref, users_ref, embed_ref, gain_ref, out_ref, assign_ref, named_ref, embed_out, gain_out):
    embed_out[...] = embed_ref[...]
    gain_out[...] = gain_ref[...]
    me = lax.rem(lax.axis_index("tm"), window)
    total = recv_ref[window - 1].astype(jnp.float32)
    for j in range(window - 1):
        total += jnp.where(j >= me, recv_ref[j].astype(jnp.float32), 0.0)
    out_ref[...] = total
    slots, sess = assign_ref.shape
    users = users_ref[...]
    section = lax.rem(users, n_sec)
    i0 = lax.broadcasted_iota(jnp.int32, (sess, sess), 0)
    i1 = lax.broadcasted_iota(jnp.int32, (sess, sess), 1)
    section_column = jnp.sum(jnp.where(i0 == i1, section, 0), axis=1, keepdims=True)
    rank = jnp.sum(jnp.where((section_column == section) & (i0 < i1), 1, 0), axis=0, keepdims=True)
    slot = section * (slots // n_sec) + rank
    assign = lax.broadcasted_iota(jnp.int32, (slots, sess), 0) == slot
    assign_ref[...] = jnp.where(assign, 1.0, 0.0).astype(jnp.bfloat16)
    named = jnp.sum(jnp.where(assign, (users + 1).astype(jnp.float32), 0.0), axis=1, keepdims=True)
    high = jnp.floor(named * (1.0 / DIGIT))
    low = named - high * DIGIT
    lane = lax.broadcasted_iota(jnp.int32, (slots, LANES), 1)
    named_ref[...] = jnp.where(lane == 0, high, jnp.where(lane == 1, low, 0.0)).astype(jnp.bfloat16)


def pack_kernel(near_ref, got_ref, embed_ref, gain_ref, assign_ref, named_ref, out_ref):
    sess = assign_ref.shape[1]
    width = embed_ref.shape[1]
    groups = width // LANES
    t = lax.axis_index("tm")
    total = near_ref[...] + got_ref[...].astype(jnp.float32)
    data = groups * sess
    counts = DIGIT * total[data : data + 1] + total[data + 1 : data + 2]
    spot = lax.broadcasted_iota(jnp.int32, (sess, LANES), 0) + sess * lax.rem(t, LANES // sess)
    mine = spot == lax.broadcasted_iota(jnp.int32, (sess, LANES), 1)
    counts = jnp.sum(jnp.where(mine, counts, 0.0), axis=1, keepdims=True)
    least = jnp.maximum(counts, 1.0)
    weight = jnp.log1p(counts)
    mixed = [
        total[g * sess : (g + 1) * sess] / least + weight * embed_ref[:, g * LANES : (g + 1) * LANES]
        for g in range(groups)
    ]
    square = sum(m * m for m in mixed)
    scale = lax.rsqrt(jnp.sum(square, axis=1, keepdims=True) / width + 1e-06)
    for g, m in enumerate(mixed):
        at = slice(g * LANES, (g + 1) * LANES)
        row = (m * scale * gain_ref[:, at]).astype(jnp.bfloat16)
        out_ref[:, at] = jnp.dot(assign_ref[...], row, preferred_element_type=jnp.float32).astype(jnp.bfloat16)
    out_ref[:, width:] = named_ref[...]


def unpack_kernel(got_ref, rows_ref, users_ref):
    slots = got_ref.shape[0]
    width = rows_ref.shape[1]
    rows_ref[...] = got_ref[:, :width]
    digits = got_ref[:, width:].astype(jnp.float32)
    lane = lax.broadcasted_iota(jnp.int32, digits.shape, 1)
    column = jnp.sum(jnp.where(lane == 0, DIGIT * digits, jnp.where(lane == 1, digits, 0.0)), axis=1, keepdims=True)
    eye = lax.broadcasted_iota(jnp.int32, (slots, slots), 0) == lax.broadcasted_iota(jnp.int32, (slots, slots), 1)
    users_ref[...] = jnp.sum(jnp.where(eye, column, 0.0), axis=0, keepdims=True).astype(jnp.int32) - 1


def on_device(
    events,
    w_first,
    b_first,
    w_second,
    count_embed,
    norm_gain,
    event_session,
    event_count,
    session_user,
):
    rows, width = events.shape[1:]
    sess = session_user.shape[1]
    n_tm = lax.axis_size("tm")
    n_sec = lax.axis_size("user")
    capacity = max(2, 2 * sess // n_sec)
    window = n_tm // 2
    block = width // LANES * sess + 8
    bf16, f32 = jnp.bfloat16, jnp.float32
    vmem = pl.BlockSpec(memory_space=pltpu.VMEM)
    shape = jax.ShapeDtypeStruct
    kept = pltpu.VMEM
    pin = functools.partial(pltpu.with_memory_space_constraint, memory_space=pltpu.VMEM)
    blocks, far = pl.pallas_call(
        functools.partial(embed_kernel, window, sess, 1024),
        out_shape=(kept((window, block, LANES), bf16), kept((block, LANES), bf16)),
        in_specs=[pl.BlockSpec(memory_space=pltpu.SMEM)] + [vmem] * 5,
        out_specs=(vmem, vmem),
        scratch_shapes=[
            pltpu.VMEM((rows, width), bf16),
            pltpu.VMEM(((window + 1) * sess, width), f32),
            pltpu.VMEM(((window + 1) * sess, LANES), f32),
        ],
        name="embed",
    )(event_count, events[0], w_first, b_first[None], w_second, event_session)
    groups = [[first + j for j in range(window)] for first in range(0, n_tm, window)]
    arrived = lax.all_to_all(blocks, "tm", 0, 0, tiled=True, axis_index_groups=groups)
    far = pl.pallas_call(
        functools.partial(far_kernel, window),
        out_shape=kept((block, LANES), bf16),
        in_specs=[vmem, vmem],
        out_specs=vmem,
        name="far",
    )(pin(arrived), pin(far))
    got = lax.ppermute(far, "tm", [(t, t - window) for t in range(window, n_tm)])
    slots = n_sec * capacity
    near, assign, named, embed, gain = pl.pallas_call(
        functools.partial(near_kernel, window, n_sec),
        out_shape=(
            kept((block, LANES), f32),
            kept((slots, sess), bf16),
            kept((slots, LANES), bf16),
            kept((1, width), f32),
            kept((1, width), f32),
        ),
        in_specs=[vmem] * 4,
        out_specs=[vmem] * 5,
        name="near",
    )(pin(arrived), session_user, count_embed[None], norm_gain[None])
    outgoing = pl.pallas_call(
        pack_kernel,
        out_shape=kept((slots, width + LANES), bf16),
        in_specs=[vmem] * 6,
        out_specs=vmem,
        name="pack",
    )(*map(pin, (near, got, embed, gain, assign, named)))
    routed = lax.all_to_all(
        outgoing.reshape(n_sec, capacity, width + LANES), "user", 0, 0, tiled=True
    ).reshape(n_sec * capacity, width + LANES)
    section_rows, section_users = pl.pallas_call(
        unpack_kernel,
        out_shape=(shape((n_sec * capacity, width), bf16), shape((1, n_sec * capacity), jnp.int32)),
        in_specs=[vmem],
        out_specs=(vmem, vmem),
        name="unpack",
    )(pin(routed))
    return (section_rows[None, None], section_users[None])


def solution(mesh):
    in_specs = (
        P("user", "tm", None),
        P(),
        P(),
        P(),
        P(),
        P(),
        P("user", "tm"),
        P("user", "tm"),
        P("user", "tm"),
    )
    out_specs = (P("tm", "user", None, None), P("tm", "user", None))
    return jax.shard_map(
        on_device, mesh=mesh, in_specs=in_specs, out_specs=out_specs, check_vma=False
    )
```

```python
import functools

import jax
import jax.numpy as jnp
from jax import lax
from jax.experimental import pallas as pl
from jax.experimental.pallas import tpu as pltpu
from jax.sharding import PartitionSpec as P

LANES = 128
DIGIT = 256.0


def count_tile(row):
    high = jnp.floor(row * (1.0 / DIGIT))
    low = row - high * DIGIT
    at = lax.broadcasted_iota(jnp.int32, (8, LANES), 0)
    return jnp.where(at == 0, high, jnp.where(at == 1, low, 0.0))


def gelu(x):
    half = 0.5 * x
    inner = x * (0.7978845608028654 + 0.035677408136300125 * (x * x))
    return half + half * jnp.tanh(inner)


def hidden_kernel(ev_ref, w1_ref, b1_ref, out_ref):
    h = jnp.dot(ev_ref[...], w1_ref[...], preferred_element_type=jnp.float32)
    out_ref[...] = gelu(h + b1_ref[...]).astype(jnp.bfloat16)


def sums_kernel(window, sess, count_ref, hidden_ref, w2_ref, ids_ref, out_ref, far_ref, acc, counted):
    rows, width = hidden_ref.shape[0], w2_ref.shape[1]
    groups = width // LANES
    pick = window * sess
    t = lax.axis_index("tm")
    vec = jnp.dot(hidden_ref[...], w2_ref[...], preferred_element_type=jnp.float32).astype(jnp.bfloat16)
    ids = ids_ref[...]
    far = (ids // sess) == t - window
    target = jnp.where(far, pick + ids % sess, ids % pick)
    valid = lax.broadcasted_iota(jnp.int32, ids.shape, 1) < count_ref[0, 0]
    target = jnp.where(valid, target, -1)
    total = pick + sess
    onehot = jnp.where(lax.broadcasted_iota(jnp.int32, (total, rows), 0) == target, 1.0, 0.0)
    counted[...] = jnp.broadcast_to(jnp.sum(onehot, axis=1, keepdims=True), counted.shape)
    acc[...] = jnp.dot(onehot.astype(jnp.bfloat16), vec, preferred_element_type=jnp.float32)
    per = LANES // sess
    row = lax.broadcasted_iota(jnp.int32, (LANES, LANES), 0)
    lane = lax.broadcasted_iota(jnp.int32, (LANES, LANES), 1)
    for c in range(pick // LANES):
        found = jnp.where(row == lane, counted[c * LANES : (c + 1) * LANES, :], 0.0)
        tile = count_tile(jnp.sum(found, axis=0, keepdims=True)).astype(jnp.bfloat16)
        for r in range(c * per, (c + 1) * per):
            for g in range(groups):
                out_ref[r, g * sess : (g + 1) * sess, :] = acc[
                    r * sess : (r + 1) * sess, g * LANES : (g + 1) * LANES
                ].astype(jnp.bfloat16)
            out_ref[r, groups * sess :, :] = tile
    for g in range(groups):
        far_ref[g * sess : (g + 1) * sess, :] = acc[pick:, g * LANES : (g + 1) * LANES].astype(jnp.bfloat16)
    spot = row[:sess] + sess * lax.rem(t, per)
    found = jnp.where(spot == lane[:sess], counted[pick:, :], 0.0)
    far_ref[groups * sess :, :] = count_tile(jnp.sum(found, axis=0, keepdims=True)).astype(jnp.bfloat16)


def far_kernel(window, recv_ref, far_ref, out_ref):
    me = lax.rem(lax.axis_index("tm"), window)
    total = far_ref[...].astype(jnp.float32)
    for j in range(window - 1):
        total += jnp.where(j < me, recv_ref[j].astype(jnp.float32), 0.0)
    data = total.shape[0] - 8
    out_ref[:data, :] = total[:data].astype(jnp.bfloat16)
    out_ref[data:, :] = count_tile(DIGIT * total[data : data + 1] + total[data + 1 : data + 2]).astype(jnp.bfloat16)


def near_kernel(window, n_sec, recv_ref, users_ref, embed_ref, gain_ref, out_ref, assign_ref, named_ref, embed_out, gain_out):
    embed_out[...] = embed_ref[...]
    gain_out[...] = gain_ref[...]
    me = lax.rem(lax.axis_index("tm"), window)
    total = recv_ref[window - 1].astype(jnp.float32)
    for j in range(window - 1):
        total += jnp.where(j >= me, recv_ref[j].astype(jnp.float32), 0.0)
    out_ref[...] = total
    slots, sess = assign_ref.shape
    users = users_ref[...]
    section = lax.rem(users, n_sec)
    i0 = lax.broadcasted_iota(jnp.int32, (sess, sess), 0)
    i1 = lax.broadcasted_iota(jnp.int32, (sess, sess), 1)
    section_column = jnp.sum(jnp.where(i0 == i1, section, 0), axis=1, keepdims=True)
    rank = jnp.sum(jnp.where((section_column == section) & (i0 < i1), 1, 0), axis=0, keepdims=True)
    slot = section * (slots // n_sec) + rank
    assign = lax.broadcasted_iota(jnp.int32, (slots, sess), 0) == slot
    assign_ref[...] = jnp.where(assign, 1.0, 0.0).astype(jnp.bfloat16)
    named = jnp.sum(jnp.where(assign, (users + 1).astype(jnp.float32), 0.0), axis=1, keepdims=True)
    high = jnp.floor(named * (1.0 / DIGIT))
    low = named - high * DIGIT
    lane = lax.broadcasted_iota(jnp.int32, (slots, LANES), 1)
    named_ref[...] = jnp.where(lane == 0, high, jnp.where(lane == 1, low, 0.0)).astype(jnp.bfloat16)


def pack_kernel(near_ref, got_ref, embed_ref, gain_ref, assign_ref, named_ref, out_ref):
    sess = assign_ref.shape[1]
    width = embed_ref.shape[1]
    groups = width // LANES
    t = lax.axis_index("tm")
    total = near_ref[...] + got_ref[...].astype(jnp.float32)
    data = groups * sess
    counts = DIGIT * total[data : data + 1] + total[data + 1 : data + 2]
    spot = lax.broadcasted_iota(jnp.int32, (sess, LANES), 0) + sess * lax.rem(t, LANES // sess)
    mine = spot == lax.broadcasted_iota(jnp.int32, (sess, LANES), 1)
    counts = jnp.sum(jnp.where(mine, counts, 0.0), axis=1, keepdims=True)
    least = jnp.maximum(counts, 1.0)
    weight = jnp.log1p(counts)
    mixed = [
        total[g * sess : (g + 1) * sess] / least + weight * embed_ref[:, g * LANES : (g + 1) * LANES]
        for g in range(groups)
    ]
    square = sum(m * m for m in mixed)
    scale = lax.rsqrt(jnp.sum(square, axis=1, keepdims=True) / width + 1e-06)
    for g, m in enumerate(mixed):
        at = slice(g * LANES, (g + 1) * LANES)
        row = (m * scale * gain_ref[:, at]).astype(jnp.bfloat16)
        out_ref[:, at] = jnp.dot(assign_ref[...], row, preferred_element_type=jnp.float32).astype(jnp.bfloat16)
    out_ref[:, width:] = named_ref[...]


def unpack_kernel(got_ref, rows_ref, users_ref):
    slots = got_ref.shape[0]
    width = rows_ref.shape[1]
    rows_ref[...] = got_ref[:, :width]
    digits = got_ref[:, width:].astype(jnp.float32)
    lane = lax.broadcasted_iota(jnp.int32, digits.shape, 1)
    column = jnp.sum(jnp.where(lane == 0, DIGIT * digits, jnp.where(lane == 1, digits, 0.0)), axis=1, keepdims=True)
    eye = lax.broadcasted_iota(jnp.int32, (slots, slots), 0) == lax.broadcasted_iota(jnp.int32, (slots, slots), 1)
    users_ref[...] = jnp.sum(jnp.where(eye, column, 0.0), axis=0, keepdims=True).astype(jnp.int32) - 1


def on_device(
    events,
    w_first,
    b_first,
    w_second,
    count_embed,
    norm_gain,
    event_session,
    event_count,
    session_user,
):
    rows, width = events.shape[1:]
    sess = session_user.shape[1]
    n_tm = lax.axis_size("tm")
    n_sec = lax.axis_size("user")
    capacity = max(2, 2 * sess // n_sec)
    window = n_tm // 2
    block = width // LANES * sess + 8
    bf16, f32 = jnp.bfloat16, jnp.float32
    vmem = pl.BlockSpec(memory_space=pltpu.VMEM)
    here = functools.partial(pltpu.with_memory_space_constraint, memory_space=pltpu.HBM)
    shape = jax.ShapeDtypeStruct
    kept = pltpu.VMEM
    pin = functools.partial(pltpu.with_memory_space_constraint, memory_space=pltpu.VMEM)
    units = w_first.shape[1]
    grant = pltpu.CompilerParams(vmem_limit_bytes=24 * 1024 * 1024)
    hidden = pl.pallas_call(
        hidden_kernel,
        out_shape=kept((rows, units), bf16),
        in_specs=[vmem] * 3,
        out_specs=vmem,
        compiler_params=grant,
        cost_estimate=pl.CostEstimate(
            flops=2 * rows * width * units, transcendentals=rows * units, bytes_accessed=2 * width * (rows + units)
        ),
        name="hidden",
    )(*map(here, (events[0], w_first, b_first[None])))
    blocks, far = pl.pallas_call(
        functools.partial(sums_kernel, window, sess),
        out_shape=(kept((window, block, LANES), bf16), kept((block, LANES), bf16)),
        in_specs=[pl.BlockSpec(memory_space=pltpu.SMEM)] + [vmem] * 3,
        out_specs=(vmem, vmem),
        scratch_shapes=[
            pltpu.VMEM(((window + 1) * sess, width), f32),
            pltpu.VMEM(((window + 1) * sess, LANES), f32),
        ],
        compiler_params=grant,
        name="sums",
    )(event_count, *map(pin, (hidden, w_second, event_session)))
    groups = [[first + j for j in range(window)] for first in range(0, n_tm, window)]
    arrived = lax.all_to_all(blocks, "tm", 0, 0, tiled=True, axis_index_groups=groups)
    far = pl.pallas_call(
        functools.partial(far_kernel, window),
        out_shape=kept((block, LANES), bf16),
        in_specs=[vmem, vmem],
        out_specs=vmem,
        name="far",
    )(pin(arrived), pin(far))
    got = lax.ppermute(far, "tm", [(t, t - window) for t in range(window, n_tm)])
    slots = n_sec * capacity
    near, assign, named, embed, gain = pl.pallas_call(
        functools.partial(near_kernel, window, n_sec),
        out_shape=(
            kept((block, LANES), f32),
            kept((slots, sess), bf16),
            kept((slots, LANES), bf16),
            kept((1, width), f32),
            kept((1, width), f32),
        ),
        in_specs=[vmem] * 4,
        out_specs=[vmem] * 5,
        name="near",
    )(pin(arrived), session_user, count_embed[None], norm_gain[None])
    outgoing = pl.pallas_call(
        pack_kernel,
        out_shape=kept((slots, width + LANES), bf16),
        in_specs=[vmem] * 6,
        out_specs=vmem,
        name="pack",
    )(*map(pin, (near, got, embed, gain, assign, named)))
    routed = lax.all_to_all(
        outgoing.reshape(n_sec, capacity, width + LANES), "user", 0, 0, tiled=True
    ).reshape(n_sec * capacity, width + LANES)
    section_rows, section_users = pl.pallas_call(
        unpack_kernel,
        out_shape=(shape((n_sec * capacity, width), bf16), shape((1, n_sec * capacity), jnp.int32)),
        in_specs=[vmem],
        out_specs=(vmem, vmem),
        name="unpack",
    )(pin(routed))
    return (section_rows[None, None], section_users[None])


def solution(mesh):
    in_specs = (
        P("user", "tm", None),
        P(),
        P(),
        P(),
        P(),
        P(),
        P("user", "tm"),
        P("user", "tm"),
        P("user", "tm"),
    )
    out_specs = (P("tm", "user", None, None), P("tm", "user", None))
    return jax.shard_map(
        on_device, mesh=mesh, in_specs=in_specs, out_specs=out_specs, check_vma=False
    )
```

```python
import functools

import jax
import jax.numpy as jnp
from jax import lax
from jax.experimental import pallas as pl
from jax.experimental.pallas import tpu as pltpu
from jax.sharding import PartitionSpec as P

LANES = 128
DIGIT = 256.0


def count_tile(row):
    high = jnp.floor(row * (1.0 / DIGIT))
    low = row - high * DIGIT
    at = lax.broadcasted_iota(jnp.int32, (8, LANES), 0)
    return jnp.where(at == 0, high, jnp.where(at == 1, low, 0.0))


def gelu(x):
    half = 0.5 * x
    inner = x * (0.7978845608028654 + 0.035677408136300125 * (x * x))
    return half + half * jnp.tanh(inner)


def embed_kernel(window, sess, step, count_ref, ev_hbm, w1_hbm, b1_hbm, w2_hbm, ids_hbm, out_ref, far_ref, vec, acc, counted, ev_ref, w1_ref, b1_ref, w2_ref, ids_ref, hidden, sems):
    half = ev_ref.shape[0] // 2
    parts = [pl.ds(k * half, half) for k in range(2)]
    pairs = [(w1_hbm, w1_ref), (b1_hbm, b1_ref), (ev_hbm.at[parts[0], :], ev_ref.at[parts[0], :])]
    pairs += [(ev_hbm.at[parts[1], :], ev_ref.at[parts[1], :]), (w2_hbm, w2_ref), (ids_hbm, ids_ref)]
    loads = [pltpu.make_async_copy(src, dst, sems.at[k]) for k, (src, dst) in enumerate(pairs)]
    for load in loads:
        load.start()
    rows, width = ev_ref.shape
    groups = width // LANES
    pick = window * sess
    t = lax.axis_index("tm")
    for part, waits in zip(parts, (loads[:3], loads[3:4])):
        for load in waits:
            load.wait()
        h = jnp.dot(ev_ref[part, :], w1_ref[...], preferred_element_type=jnp.float32)
        hidden[part, :] = gelu(h + b1_ref[...]).astype(jnp.bfloat16)
    for load in loads[4:]:
        load.wait()
    vec[...] = jnp.dot(hidden[...], w2_ref[...], preferred_element_type=jnp.float32).astype(jnp.bfloat16)
    ids = ids_ref[...]
    far = (ids // sess) == t - window
    target = jnp.where(far, pick + ids % sess, ids % pick)
    valid = lax.broadcasted_iota(jnp.int32, ids.shape, 1) < count_ref[0, 0]
    target = jnp.where(valid, target, -1)
    total = pick + sess
    onehot = jnp.where(lax.broadcasted_iota(jnp.int32, (total, rows), 0) == target, 1.0, 0.0)
    counted[...] = jnp.broadcast_to(jnp.sum(onehot, axis=1, keepdims=True), counted.shape)
    acc[...] = jnp.dot(onehot.astype(jnp.bfloat16), vec[...], preferred_element_type=jnp.float32)
    per = LANES // sess
    row = lax.broadcasted_iota(jnp.int32, (LANES, LANES), 0)
    lane = lax.broadcasted_iota(jnp.int32, (LANES, LANES), 1)
    for c in range(pick // LANES):
        found = jnp.where(row == lane, counted[c * LANES : (c + 1) * LANES, :], 0.0)
        tile = count_tile(jnp.sum(found, axis=0, keepdims=True)).astype(jnp.bfloat16)
        for r in range(c * per, (c + 1) * per):
            for g in range(groups):
                out_ref[r, g * sess : (g + 1) * sess, :] = acc[
                    r * sess : (r + 1) * sess, g * LANES : (g + 1) * LANES
                ].astype(jnp.bfloat16)
            out_ref[r, groups * sess :, :] = tile
    for g in range(groups):
        far_ref[g * sess : (g + 1) * sess, :] = acc[pick:, g * LANES : (g + 1) * LANES].astype(jnp.bfloat16)
    spot = row[:sess] + sess * lax.rem(t, per)
    found = jnp.where(spot == lane[:sess], counted[pick:, :], 0.0)
    far_ref[groups * sess :, :] = count_tile(jnp.sum(found, axis=0, keepdims=True)).astype(jnp.bfloat16)


def far_kernel(window, recv_ref, far_ref, out_ref):
    me = lax.rem(lax.axis_index("tm"), window)
    total = far_ref[...].astype(jnp.float32)
    for j in range(window - 1):
        total += jnp.where(j < me, recv_ref[j].astype(jnp.float32), 0.0)
    data = total.shape[0] - 8
    out_ref[:data, :] = total[:data].astype(jnp.bfloat16)
    out_ref[data:, :] = count_tile(DIGIT * total[data : data + 1] + total[data + 1 : data + 2]).astype(jnp.bfloat16)


def near_kernel(window, n_sec, recv_ref, users_ref, embed_ref, gain_ref, out_ref, assign_ref, named_ref, embed_out, gain_out):
    embed_out[...] = embed_ref[...]
    gain_out[...] = gain_ref[...]
    me = lax.rem(lax.axis_index("tm"), window)
    total = recv_ref[window - 1].astype(jnp.float32)
    for j in range(window - 1):
        total += jnp.where(j >= me, recv_ref[j].astype(jnp.float32), 0.0)
    out_ref[...] = total
    slots, sess = assign_ref.shape
    users = users_ref[...]
    section = lax.rem(users, n_sec)
    i0 = lax.broadcasted_iota(jnp.int32, (sess, sess), 0)
    i1 = lax.broadcasted_iota(jnp.int32, (sess, sess), 1)
    section_column = jnp.sum(jnp.where(i0 == i1, section, 0), axis=1, keepdims=True)
    rank = jnp.sum(jnp.where((section_column == section) & (i0 < i1), 1, 0), axis=0, keepdims=True)
    slot = section * (slots // n_sec) + rank
    assign = lax.broadcasted_iota(jnp.int32, (slots, sess), 0) == slot
    assign_ref[...] = jnp.where(assign, 1.0, 0.0).astype(jnp.bfloat16)
    named = jnp.sum(jnp.where(assign, (users + 1).astype(jnp.float32), 0.0), axis=1, keepdims=True)
    high = jnp.floor(named * (1.0 / DIGIT))
    low = named - high * DIGIT
    lane = lax.broadcasted_iota(jnp.int32, (slots, LANES), 1)
    named_ref[...] = jnp.where(lane == 0, high, jnp.where(lane == 1, low, 0.0)).astype(jnp.bfloat16)


def pack_kernel(near_ref, got_ref, embed_ref, gain_ref, assign_ref, named_ref, out_ref):
    sess = assign_ref.shape[1]
    width = embed_ref.shape[1]
    groups = width // LANES
    t = lax.axis_index("tm")
    total = near_ref[...] + got_ref[...].astype(jnp.float32)
    data = groups * sess
    counts = DIGIT * total[data : data + 1] + total[data + 1 : data + 2]
    spot = lax.broadcasted_iota(jnp.int32, (sess, LANES), 0) + sess * lax.rem(t, LANES // sess)
    mine = spot == lax.broadcasted_iota(jnp.int32, (sess, LANES), 1)
    counts = jnp.sum(jnp.where(mine, counts, 0.0), axis=1, keepdims=True)
    least = jnp.maximum(counts, 1.0)
    weight = jnp.log1p(counts)
    mixed = [
        total[g * sess : (g + 1) * sess] / least + weight * embed_ref[:, g * LANES : (g + 1) * LANES]
        for g in range(groups)
    ]
    square = sum(m * m for m in mixed)
    scale = lax.rsqrt(jnp.sum(square, axis=1, keepdims=True) / width + 1e-06)
    for g, m in enumerate(mixed):
        at = slice(g * LANES, (g + 1) * LANES)
        row = (m * scale * gain_ref[:, at]).astype(jnp.bfloat16)
        out_ref[:, at] = jnp.dot(assign_ref[...], row, preferred_element_type=jnp.float32).astype(jnp.bfloat16)
    out_ref[:, width:] = named_ref[...]


def unpack_kernel(got_ref, rows_ref, users_ref):
    slots = got_ref.shape[0]
    width = rows_ref.shape[1]
    rows_ref[...] = got_ref[:, :width]
    digits = got_ref[:, width:].astype(jnp.float32)
    lane = lax.broadcasted_iota(jnp.int32, digits.shape, 1)
    column = jnp.sum(jnp.where(lane == 0, DIGIT * digits, jnp.where(lane == 1, digits, 0.0)), axis=1, keepdims=True)
    eye = lax.broadcasted_iota(jnp.int32, (slots, slots), 0) == lax.broadcasted_iota(jnp.int32, (slots, slots), 1)
    users_ref[...] = jnp.sum(jnp.where(eye, column, 0.0), axis=0, keepdims=True).astype(jnp.int32) - 1


def on_device(
    events,
    w_first,
    b_first,
    w_second,
    count_embed,
    norm_gain,
    event_session,
    event_count,
    session_user,
):
    rows, width = events.shape[1:]
    sess = session_user.shape[1]
    n_tm = lax.axis_size("tm")
    n_sec = lax.axis_size("user")
    capacity = max(2, 2 * sess // n_sec)
    window = n_tm // 2
    block = width // LANES * sess + 8
    bf16, f32 = jnp.bfloat16, jnp.float32
    vmem = pl.BlockSpec(memory_space=pltpu.VMEM)
    hbm = pl.BlockSpec(memory_space=pltpu.HBM)
    here = functools.partial(pltpu.with_memory_space_constraint, memory_space=pltpu.HBM)
    shape = jax.ShapeDtypeStruct
    kept = pltpu.VMEM
    pin = functools.partial(pltpu.with_memory_space_constraint, memory_space=pltpu.VMEM)
    blocks, far = pl.pallas_call(
        functools.partial(embed_kernel, window, sess, 1024),
        out_shape=(kept((window, block, LANES), bf16), kept((block, LANES), bf16)),
        in_specs=[pl.BlockSpec(memory_space=pltpu.SMEM)] + [hbm] * 5,
        out_specs=(vmem, vmem),
        scratch_shapes=[
            pltpu.VMEM((rows, width), bf16),
            pltpu.VMEM(((window + 1) * sess, width), f32),
            pltpu.VMEM(((window + 1) * sess, LANES), f32),
            pltpu.VMEM((rows, width), bf16),
            pltpu.VMEM(w_first.shape, bf16),
            pltpu.VMEM((1, w_first.shape[1]), f32),
            pltpu.VMEM(w_second.shape, bf16),
            pltpu.VMEM((1, rows), jnp.int32),
            pltpu.VMEM((rows, w_first.shape[1]), bf16),
            pltpu.SemaphoreType.DMA((6,)),
        ],
        name="embed",
    )(event_count, *map(here, (events[0], w_first, b_first[None], w_second, event_session)))
    groups = [[first + j for j in range(window)] for first in range(0, n_tm, window)]
    arrived = lax.all_to_all(blocks, "tm", 0, 0, tiled=True, axis_index_groups=groups)
    far = pl.pallas_call(
        functools.partial(far_kernel, window),
        out_shape=kept((block, LANES), bf16),
        in_specs=[vmem, vmem],
        out_specs=vmem,
        name="far",
    )(pin(arrived), pin(far))
    got = lax.ppermute(far, "tm", [(t, t - window) for t in range(window, n_tm)])
    slots = n_sec * capacity
    near, assign, named, embed, gain = pl.pallas_call(
        functools.partial(near_kernel, window, n_sec),
        out_shape=(
            kept((block, LANES), f32),
            kept((slots, sess), bf16),
            kept((slots, LANES), bf16),
            kept((1, width), f32),
            kept((1, width), f32),
        ),
        in_specs=[vmem] * 4,
        out_specs=[vmem] * 5,
        name="near",
    )(pin(arrived), session_user, count_embed[None], norm_gain[None])
    outgoing = pl.pallas_call(
        pack_kernel,
        out_shape=kept((slots, width + LANES), bf16),
        in_specs=[vmem] * 6,
        out_specs=vmem,
        name="pack",
    )(*map(pin, (near, got, embed, gain, assign, named)))
    routed = lax.all_to_all(
        outgoing.reshape(n_sec, capacity, width + LANES), "user", 0, 0, tiled=True
    ).reshape(n_sec * capacity, width + LANES)
    section_rows, section_users = pl.pallas_call(
        unpack_kernel,
        out_shape=(shape((n_sec * capacity, width), bf16), shape((1, n_sec * capacity), jnp.int32)),
        in_specs=[vmem],
        out_specs=(vmem, vmem),
        name="unpack",
    )(pin(routed))
    return (section_rows[None, None], section_users[None])


def solution(mesh):
    in_specs = (
        P("user", "tm", None),
        P(),
        P(),
        P(),
        P(),
        P(),
        P("user", "tm"),
        P("user", "tm"),
        P("user", "tm"),
    )
    out_specs = (P("tm", "user", None, None), P("tm", "user", None))
    return jax.shard_map(
        on_device, mesh=mesh, in_specs=in_specs, out_specs=out_specs, check_vma=False
    )
```
